32 devices in a mesh: groups: 2 (over y), tensor: 4 (over z), seq: 2 (over core), dp: 2 (over x).
Axes of the slice: x: 2, y: 2, z: 4, core: 2. Of those that a mesh axis runs over, the one named last changes fastest.
Arguments:
- queries: bfloat16 [4, 512, 8192], P(('groups', 'dp'), 'seq', 'tensor'), parts along dimension 0, may hold values from -120 to 120
- stretch_keys: bfloat16 [4, 512, 4096], P(('groups', 'dp'), 'seq', 'tensor'), parts along dimension 0, may hold values from -5 to 5
- stretch_values: bfloat16 [4, 512, 4096], P(('groups', 'dp'), 'seq', 'tensor'), parts along dimension 0, may hold values from -96 to 96
- cache_keys: bfloat16 [4, 3584, 4096], P(('groups', 'dp'), 'seq', 'tensor'), parts along dimension 0, may hold values from -5 to 5
- cache_values: bfloat16 [4, 3584, 4096], P(('groups', 'dp'), 'seq', 'tensor'), parts along dimension 0, may hold values from -96 to 96
- blocks: bfloat16 [64, 32, 128, 128], P('tensor', 'dp'), may hold values from -0.09375 to 0.09375
- block_columns: int32 [64, 32], P('tensor', 'dp'), may hold values from 0 to 63, as said below
Outputs:
- projected: bfloat16 [4, 512, 8192], P(('groups', 'dp'), 'seq', 'tensor'), parts along dimension 0
The draws below stay inside these ranges and needn't reach their ends.
There are 2 independent parts, one for each index of `groups`. The reference program is written for one: setup_inputs(seed, part) draws one part's arguments, and reference() takes and returns one part's arrays. A program takes and returns all parts, laid end to end along the dimension named above; an argument that names none is the same for every part. Nothing has to cross between parts.
Inputs may be any that keep to these rules, and one draw needn't show every extreme that they name: `block_columns`: each row of blocks lists 32 different column blocks.
All inputs are finite; a program needn't handle non-finite values.
Results may differ from the reference program's by a relative error of at most 0.02.
Values may be sent and summed in bfloat16 or wider, within the bound.
No kernel may reach another device: no remote copies, remote signals or barrier semaphores. Data moves between devices by JAX's collectives and lax.ppermute only.
A program may use at most 256 MiB of HBM per device.

```python
import jax
import jax.numpy as jnp
from jax import lax

D = 8192
HD = 128
BS = 128
KW = 4096
KEEP = 32
SEQS = 2
LEN = 512
PREV = 3584
N_TENSOR = 4


def attention_tables(key):
    query_key = jax.random.fold_in(key, 101)
    cache_key = jax.random.fold_in(key, 202)
    key_table = jnp.clip(jax.random.normal(cache_key, (SEQS, PREV, KW), jnp.float32), -5.0, 5.0)
    query_table = jnp.clip(jax.random.normal(query_key, (SEQS, LEN, D), jnp.float32), -4.5, 4.5)
    return (query_table, key_table)


def draw_queries(key, part):
    return attention_tables(key)[0].astype(jnp.bfloat16)


def draw_cache_keys(key, part):
    return attention_tables(key)[1].astype(jnp.bfloat16)


def draw_block_columns(key, part):
    col_count = D // BS
    noise_draw = jax.random.randint(jax.random.fold_in(key, 7), (D // BS, col_count), 0, 1 << 20)
    favour = jax.random.randint(jax.random.fold_in(key, 8), (col_count,), 0, 1 << 19)
    ranked = (noise_draw + favour[None, :]) * col_count + jnp.arange(col_count)[None, :]
    return lax.top_k(ranked, KEEP)[1].astype(jnp.int32)


def block_levels(key, dims, shards, low, high):
    def one(position, parts):
        draws = jax.random.uniform(jax.random.fold_in(jax.random.fold_in(key, 6), position), (parts,), jnp.float32, low / len(shards), high / len(shards))
        return jnp.repeat(jnp.exp(draws), dims[position] // parts).reshape((-1,) + (1,) * (len(dims) - position - 1))

    level = one(*shards[0])
    for cut in shards[1:]:
        level = level * one(*cut)
    return level


def scatter_about(stream_key, extent, scale, most, pieces=(), held_as=jnp.bfloat16):
    loudness = block_levels(stream_key, extent, pieces, -0.22, 0.18) if pieces else 1.0
    values = jax.random.normal(stream_key, extent, jnp.float32) * scale * loudness
    return jnp.minimum(jnp.maximum(values, -most), most).astype(held_as)


def setup_inputs(seed: int = 0, part: int = 0) -> dict:
    seeds = jax.random.split(jax.random.key(seed), 8)
    part_splits = jax.random.split(jax.random.fold_in(seeds[7], part), 8)
    queries = draw_queries(jax.random.fold_in(jax.random.fold_in(seeds[7], part), 71), part)
    stretch_keys = scatter_about(part_splits[1], (SEQS, LEN, KW), 1.0, 5.0, ((0, 2), (1, 2), (2, 4)))
    stretch_values = scatter_about(part_splits[2], (SEQS, LEN, KW), 16.0, 96.0, ((0, 2), (1, 2), (2, 4)))
    cache_keys = draw_cache_keys(jax.random.fold_in(jax.random.fold_in(seeds[7], part), 71), part)
    cache_values = scatter_about(part_splits[4], (SEQS, PREV, KW), 16.0, 96.0, ((0, 2), (1, 2), (2, 4)))
    blocks = scatter_about(seeds[5], (D // BS, KEEP, BS, BS), (D // 2) ** -0.5, 0.09375, ((0, 4), (1, 2)))
    block_columns = draw_block_columns(jax.random.fold_in(seeds[7], 71), part)
    return {"queries": queries, "stretch_keys": stretch_keys, "stretch_values": stretch_values, "cache_keys": cache_keys, "cache_values": cache_values, "blocks": blocks, "block_columns": block_columns}


floor_score = -1.0e30


def attend_pair(query_pair, key_head, value_head):
    scores = jnp.einsum("tgd,md->gtm", query_pair.astype(jnp.float32), key_head.astype(jnp.float32), precision=lax.Precision.HIGHEST) * (HD ** -0.5)
    query_pos = jnp.arange(LEN)
    key_pos = jnp.arange(PREV + LEN)
    visible = (key_pos[None, :] < PREV) | (key_pos[None, :] - PREV <= query_pos[:, None])
    scores = jnp.where(visible[None], scores, floor_score)
    peak = jnp.max(scores, axis=-1, keepdims=True)
    expo = jnp.where(visible[None], jnp.exp(scores - peak), 0.0)
    totals = jnp.sum(expo, axis=-1)
    expo_b = expo.astype(jnp.bfloat16).astype(jnp.float32)
    summed = jnp.einsum("gtm,md->tgd", expo_b, value_head.astype(jnp.float32), precision=lax.Precision.HIGHEST)
    return summed / jnp.moveaxis(totals, 0, 1)[..., None]


def reference(queries, stretch_keys, stretch_values, cache_keys, cache_values, blocks, block_columns):
    key_heads = KW // HD
    context_keys = jnp.concatenate([cache_keys, stretch_keys], axis=1).reshape(SEQS, PREV + LEN, key_heads, HD)
    context_values = jnp.concatenate([cache_values, stretch_values], axis=1).reshape(SEQS, PREV + LEN, key_heads, HD)
    query_heads = queries.reshape(SEQS, LEN, key_heads, 2, HD)

    def one_sequence(items):
        query_seq, key_seq, value_seq = items

        def one_head(head_items):
            return attend_pair(head_items[0], head_items[1], head_items[2])

        outcome = lax.map(one_head, (jnp.moveaxis(query_seq, 1, 0), jnp.moveaxis(key_seq, 1, 0), jnp.moveaxis(value_seq, 1, 0)))
        return jnp.moveaxis(outcome, 0, 1).reshape(LEN, D)

    attended = lax.map(one_sequence, (query_heads, context_keys, context_values)).astype(jnp.bfloat16)
    tokens_all = SEQS * LEN
    row_groups = jnp.moveaxis(attended.reshape(tokens_all, N_TENSOR, -1, BS), 1, 0)
    group_blocks = blocks.reshape(N_TENSOR, -1, KEEP, BS, BS)
    group_columns = block_columns.reshape(N_TENSOR, -1, KEEP)

    def add_group(running, items):
        x_group, w_group, c_group = items
        product = jnp.einsum("trk,rmkn->trmn", x_group.astype(jnp.float32), w_group.astype(jnp.float32), precision=lax.Precision.HIGHEST)
        term = jnp.zeros((tokens_all, D // BS, BS), jnp.float32)
        term = term.at[:, c_group.reshape(-1)].add(product.reshape(tokens_all, -1, BS))
        rounded = lax.optimization_barrier(term.reshape(tokens_all, D).astype(jnp.bfloat16))
        return running + rounded.astype(jnp.float32), None

    summed, _ = lax.scan(add_group, jnp.zeros((tokens_all, D), jnp.float32), (row_groups, group_blocks, group_columns))
    return summed.astype(jnp.bfloat16).reshape(SEQS, LEN, D)
```

```python
import functools
import math

import jax
import jax.numpy as jnp
from jax import lax
from jax.experimental import pallas as pl
from jax.experimental.pallas import tpu as pltpu
from jax.sharding import PartitionSpec as P

HD = 128
FLOOR = -1e30
TILE = 1024


def attention_body(seq_ref, q_ref, cka_ref, ska_ref, ckb_ref, skb_ref, cva_ref, sva_ref, cvb_ref, svb_ref, out_ref):
    rows = q_ref.shape[0]
    scale = HD ** (-0.5) * math.log2(math.e)
    q = q_ref[...].astype(jnp.float32) * scale
    q_hi = q.astype(jnp.bfloat16)
    q_lo = (q - q_hi.astype(jnp.float32)).astype(jnp.bfloat16)
    q_two = jnp.concatenate(
        [jnp.concatenate([q_hi[:, h * HD : (h + 1) * HD], q_lo[:, h * HD : (h + 1) * HD]], axis=1) for h in range(2)],
        axis=0,
    )
    tiles = []
    for side, (ck, sk, cv, sv) in enumerate(
        ((cka_ref, ska_ref, cva_ref, sva_ref), (ckb_ref, skb_ref, cvb_ref, svb_ref))
    ):
        cache_rows = ck.shape[0]
        whole = cache_rows // TILE
        for t in range(whole):
            tiles.append((ck[t * TILE : (t + 1) * TILE, :], cv[t * TILE : (t + 1) * TILE, :], None))
        tiles.append(
            (
                jnp.concatenate([ck[whole * TILE :, :], sk[...]], axis=0),
                jnp.concatenate([cv[whole * TILE :, :], sv[...]], axis=0),
                side,
            )
        )
    peak = None
    acc = None
    for keys, values, side in tiles:
        scores = lax.dot_general(
            q_two,
            jnp.concatenate([keys, keys], axis=1),
            (((1,), (1,)), ((), ())),
            preferred_element_type=jnp.float32,
        )
        if side is not None:
            plain = scores.shape[1] - rows
            tail = scores[:, plain:]
            if side == 0:
                token = lax.broadcasted_iota(jnp.int32, (rows, rows), 0)
                position = lax.broadcasted_iota(jnp.int32, (rows, rows), 1)
                seen = position <= token
                seen = jnp.concatenate([seen, seen], axis=0)
                tail = jnp.where(seen, tail, FLOOR)
            else:
                tail = jnp.where(seq_ref[0] > 0, tail, FLOOR)
            scores = jnp.concatenate([scores[:, :plain], tail], axis=1)
        tile_peak = jnp.max(scores, axis=1, keepdims=True)
        new_peak = tile_peak if peak is None else jnp.maximum(peak, tile_peak)
        expo = jnp.exp2(scores - new_peak).astype(jnp.bfloat16)
        added = jnp.dot(
            expo,
            jnp.concatenate([values, jnp.ones_like(values)], axis=1),
            preferred_element_type=jnp.float32,
        )
        acc = added if acc is None else acc * jnp.exp2(peak - new_peak) + added
        peak = new_peak
    result = acc[:, :HD] / acc[:, HD:]
    out_ref[:, :HD] = result[:rows].astype(out_ref.dtype)
    out_ref[:, HD:] = result[rows:].astype(out_ref.dtype)


def attention(my_seq, q, own, peer):
    rows, width = q.shape
    cache_rows = own[0].shape[0]
    heads = width // (2 * HD)
    qspec = pl.BlockSpec((rows, 2 * HD), lambda g, s: (0, g))
    cspec = pl.BlockSpec((cache_rows, HD), lambda g, s: (0, g))
    nspec = pl.BlockSpec((rows, HD), lambda g, s: (0, g))
    total = 2 * (cache_rows + rows)
    return pl.pallas_call(
        attention_body,
        out_shape=jax.ShapeDtypeStruct((rows, width), jnp.bfloat16),
        grid_spec=pltpu.PrefetchScalarGridSpec(
            num_scalar_prefetch=1,
            grid=(heads,),
            in_specs=[qspec, cspec, nspec, cspec, nspec, cspec, nspec, cspec, nspec],
            out_specs=qspec,
        ),
        compiler_params=pltpu.CompilerParams(
            dimension_semantics=("arbitrary",), vmem_limit_bytes=56 << 20
        ),
        cost_estimate=pl.CostEstimate(
            flops=8 * heads * rows * total * HD,
            transcendentals=2 * heads * rows * total,
            bytes_accessed=4 * (total * heads * HD + rows * width),
        ),
        name="attention",
    )(my_seq, q, own[0], own[1], peer[0], peer[1], own[2], own[3], peer[2], peer[3])


def projection_body(n_pieces, step_cols, table_ref, start_ref, x_ref, *refs):
    pieces = refs[:n_pieces]
    out_ref, held, sems = refs[n_pieces:]
    rows = x_ref.shape[1] // HD
    offset = 0
    copies = []
    for i, piece in enumerate(pieces):
        count = piece.shape[0]
        copies.append(
            pltpu.make_async_copy(piece, held.at[pl.ds(start_ref[i], count)], sems.at[i])
        )
        offset += count

    @pl.when(pl.program_id(0) == 0)
    def _():
        for copy in copies:
            copy.start()
        held[offset] = jnp.zeros(held.shape[1:], held.dtype)
        for copy in copies:
            copy.wait()

    base = pl.program_id(0) * step_cols
    x = x_ref[...]
    for pair in range(step_cols // 2):
        sides = []
        for side in range(2):
            col = base + 2 * pair + side
            sides.append(jnp.concatenate([held[table_ref[r, col]] for r in range(rows)], axis=0))
        panel = jnp.concatenate(sides, axis=1)
        value = jnp.dot(x, panel, preferred_element_type=jnp.float32)
        out_ref[:, 2 * pair * HD : 2 * (pair + 1) * HD] = value.astype(out_ref.dtype)


def projection(x, table, starts, pieces, col_blocks):
    tokens, width = x.shape
    step_cols = 8
    total = sum(p.shape[0] for p in pieces)
    return pl.pallas_call(
        functools.partial(projection_body, len(pieces), step_cols),
        out_shape=jax.ShapeDtypeStruct((tokens, col_blocks * HD), jnp.bfloat16),
        grid_spec=pltpu.PrefetchScalarGridSpec(
            num_scalar_prefetch=2,
            grid=(col_blocks // step_cols,),
            in_specs=[pl.BlockSpec((tokens, width), lambda n, t, s: (0, 0))]
            + [pl.BlockSpec(memory_space=pl.ANY)] * len(pieces),
            out_specs=pl.BlockSpec((tokens, step_cols * HD), lambda n, t, s: (0, n)),
            scratch_shapes=[
                pltpu.VMEM((total + 1, HD, HD), jnp.bfloat16),
                pltpu.SemaphoreType.DMA((len(pieces),)),
            ],
        ),
        compiler_params=pltpu.CompilerParams(
            dimension_semantics=("arbitrary",), vmem_limit_bytes=56 << 20
        ),
        cost_estimate=pl.CostEstimate(
            flops=2 * tokens * width * col_blocks * HD,
            transcendentals=0,
            bytes_accessed=2 * (total * HD * HD + tokens * width + tokens * col_blocks * HD),
        ),
        name="projection",
    )(table, starts, x, *pieces)


def swap(value, axis):
    return lax.ppermute(value, axis, [(0, 1), (1, 0)])


def shards(mesh, queries, stretch_keys, stretch_values, cache_keys, cache_values, blocks, block_columns):
    tok_rows, width_dev = queries.shape[1:]
    row_blocks, kept, block_size = blocks.shape[:3]
    col_blocks = mesh.shape["tensor"] * width_dev // block_size
    my_seq = lax.axis_index("seq")

    if mesh.shape["dp"] == 2 and mesh.shape["groups"] == 2 and row_blocks % 4 == 0:
        quarter_rows = row_blocks // 4
        groups = lax.axis_index("groups")
        quarter = 2 * my_seq + groups
        quarter_of = lambda s, g: (2 * s + g) * quarter_rows * kept
        mine = lax.dynamic_slice_in_dim(blocks, quarter * quarter_rows, quarter_rows, 0)
        mine = mine.reshape(quarter_rows * kept, block_size, block_size)
        step = quarter_rows * kept // 4
        from_x = [swap(mine[i * step : (i + 1) * step], "dp") for i in range(4)]
        from_y = [swap(part, "groups") for part in from_x]
        from_core = [swap(part, "seq") for part in from_x + from_y]
        pieces = [blocks.reshape(row_blocks * kept, block_size, block_size)] + from_x + from_y + from_core
        first = row_blocks * kept
        starts = [0]
        for s, g in ((my_seq, groups), (my_seq, 1 - groups), (1 - my_seq, groups), (1 - my_seq, 1 - groups)):
            starts += [first + quarter_of(s, g) + i * step for i in range(4)]
        all_columns = jnp.stack([block_columns, swap(block_columns, "dp")])
    else:
        gathered = lax.all_gather(blocks, "dp", axis=0)
        pieces = [gathered.reshape(-1, block_size, block_size)]
        starts = [0]
        all_columns = lax.all_gather(block_columns, "dp", axis=0)
    starts = jnp.stack([jnp.int32(s) for s in starts])
    held = all_columns.size
    place = jnp.arange(held, dtype=jnp.int32).reshape(all_columns.shape)
    match = all_columns[..., None] == jnp.arange(col_blocks, dtype=jnp.int32)
    table = jnp.min(jnp.where(match, place[..., None], held), axis=(0, 2))

    own = [a[0] for a in (cache_keys, stretch_keys, cache_values, stretch_values)]
    peer = [swap(a, "seq") for a in own]
    attended = attention(my_seq.reshape(1), queries[0], own, peer)
    partial_value = projection(attended, table, starts, pieces, col_blocks)
    owned = lax.psum_scatter(partial_value, "tensor", scatter_dimension=1, tiled=True)
    return owned[None]


def solution(mesh):
    token = P(("groups", "dp"), "seq", "tensor")
    placed = (token, token, token, token, token, P("tensor", "dp", None, None), P("tensor", "dp"))
    return jax.shard_map(
        functools.partial(shards, mesh),
        mesh=mesh,
        in_specs=placed,
        out_specs=token,
        check_vma=False,
    )
```

```python
import functools
import math

import jax
import jax.numpy as jnp
from jax import lax
from jax.experimental import pallas as pl
from jax.experimental.pallas import tpu as pltpu
from jax.sharding import PartitionSpec as P

HD = 128
FLOOR = -1e30
TILE = 768
STEP_COLS = 8
EXTRA = 1


def in_hbm(value):
    return pltpu.with_memory_space_constraint(value, pltpu.HBM)


def attention_body(seq_ref, q_ref, cka, ska, ckb, skb, cva, sva, cvb, svb, out_ref):
    rows = q_ref.shape[0]
    cache_rows = cka.shape[0]
    scale = HD ** (-0.5) * math.log2(math.e)
    q = q_ref[...].astype(jnp.float32) * scale
    q_hi = q.astype(jnp.bfloat16)
    q_lo = (q - q_hi.astype(jnp.float32)).astype(jnp.bfloat16)
    q_two = jnp.concatenate(
        [jnp.concatenate([q_hi[:, h * HD : (h + 1) * HD], q_lo[:, h * HD : (h + 1) * HD]], axis=1) for h in range(2)],
        axis=0,
    )
    whole = (cache_rows - 1) // TILE
    tiles = []
    for side, (ck, sk, cv, sv) in enumerate(((cka, ska, cva, sva), (ckb, skb, cvb, svb))):
        for t in range(whole):
            tiles.append((ck, cv, None, None, t * TILE, (t + 1) * TILE, None))
        tiles.append((ck, cv, sk, sv, whole * TILE, cache_rows, side))

    def take(main, fresh, lo, hi):
        return main[lo:hi, :] if fresh is None else jnp.concatenate([main[lo:hi, :], fresh[...]], axis=0)

    def score(tile):
        ck, _, sk, _, lo, hi, side = tile
        keys = take(ck, sk, lo, hi)
        scores = lax.dot_general(
            q_two,
            jnp.concatenate([keys, keys], axis=1),
            (((1,), (1,)), ((), ())),
            preferred_element_type=jnp.float32,
        )
        if side is None:
            return scores
        tail = scores[:, hi - lo :]
        if side == 0:
            token = lax.broadcasted_iota(jnp.int32, (rows, rows), 0)
            position = lax.broadcasted_iota(jnp.int32, (rows, rows), 1)
            seen = position <= token
            tail = jnp.where(jnp.concatenate([seen, seen], axis=0), tail, FLOOR)
        else:
            tail = jnp.where(seq_ref[0] > 0, tail, FLOOR)
        return jnp.concatenate([scores[:, : hi - lo], tail], axis=1)

    peak = acc = None
    upcoming = score(tiles[0])
    for i, tile in enumerate(tiles):
        scores = upcoming
        if i + 1 < len(tiles):
            upcoming = score(tiles[i + 1])
        tile_peak = jnp.max(scores, axis=1, keepdims=True)
        new_peak = tile_peak if peak is None else jnp.maximum(peak, tile_peak)
        expo = jnp.exp2(scores - new_peak).astype(jnp.bfloat16)
        values = take(tile[1], tile[3], tile[4], tile[5])
        added = jnp.dot(
            expo,
            jnp.concatenate([values, jnp.ones_like(values)], axis=1),
            preferred_element_type=jnp.float32,
        )
        acc = added if acc is None else acc * jnp.exp2(peak - new_peak) + added
        peak = new_peak
    result = acc[:, :HD] / acc[:, HD:]
    out_ref[:, :HD] = result[:rows].astype(out_ref.dtype)
    out_ref[:, HD:] = result[rows:].astype(out_ref.dtype)


def attention(my_seq, q, own, peer, first, count, earlier=None):
    rows, width = q.shape
    ck, sk, cv, sv = own
    pck, ps, pcv = peer
    cache_rows = ck.shape[0]
    qspec = pl.BlockSpec((rows, 2 * HD), lambda g, s: (0, g + first))
    cspec = pl.BlockSpec((cache_rows, HD), lambda g, s: (0, g + first))
    nspec = pl.BlockSpec((rows, HD), lambda g, s: (0, g + first))
    vspec = pl.BlockSpec((rows, HD), lambda g, s: (1, g + first))
    args = [q, ck, sk, pck, ps, cv, sv, pcv, ps]
    specs = [qspec, cspec, nspec, cspec, nspec, cspec, nspec, cspec, vspec]
    body = attention_body
    aliases = {}
    if earlier is not None:
        body = lambda *refs: attention_body(*refs[:10], *refs[11:])
        args.append(earlier)
        specs.append(pl.BlockSpec(memory_space=pltpu.HBM))
        aliases = {10: 0}
    return pl.pallas_call(
        body,
        out_shape=pltpu.HBM((rows, width), jnp.bfloat16),
        grid_spec=pltpu.PrefetchScalarGridSpec(
            num_scalar_prefetch=1,
            grid=(count,),
            in_specs=specs,
            out_specs=qspec,
        ),
        input_output_aliases=aliases,
        compiler_params=pltpu.CompilerParams(
            dimension_semantics=("arbitrary",), vmem_limit_bytes=20 << 20
        ),
        cost_estimate=pl.CostEstimate(flops=1, transcendentals=0, bytes_accessed=1),
        name="attention" if earlier is None else "late_attention",
    )(my_seq, *[in_hbm(a) for a in args])


def projection_body(sources, kept, has_acc, table_ref, rows_ref, x_ref, *refs):
    n_pieces = 1 + max(piece for row in sources for piece, _, _ in row)
    pieces = refs[:n_pieces]
    refs = refs[n_pieces:]
    if has_acc:
        acc_hbm, refs = refs[0], refs[1:]
    out_ref, held, sems, stage, out_sems = refs[:5]
    slots = len(sources[0]) * kept
    empty = len(sources) * slots
    row_ids = [rows_ref[i] for i in range(len(sources))]
    copies = []
    for i, row in enumerate(sources):
        for j, (piece, offset, by_row) in enumerate(row):
            start = offset + row_ids[i] * kept if by_row else offset
            copies.append(
                pltpu.make_async_copy(
                    pieces[piece].at[pl.ds(start, kept)],
                    held.at[pl.ds(i * slots + j * kept, kept)],
                    sems.at[i, j],
                )
            )
    for copy in copies:
        copy.start()
    n_steps = table_ref.shape[1] // STEP_COLS
    span = STEP_COLS * HD

    def fill(step):
        acc_ref, acc_sems = refs[5:]
        where = pl.ds(pl.multiple_of(step * span, span), span)
        return pltpu.make_async_copy(acc_hbm.at[:, where], acc_ref.at[step], acc_sems.at[step])

    if has_acc:
        for step in range(n_steps):
            fill(step).start()
    held[empty] = jnp.zeros(held.shape[1:], held.dtype)
    for copy in copies:
        copy.wait()
    x = jnp.concatenate([x_ref[:, pl.ds(pl.multiple_of(r * HD, HD), HD)] for r in row_ids], axis=1)

    def drain(slot, step):
        return pltpu.make_async_copy(
            stage.at[slot], out_ref.at[:, pl.ds(pl.multiple_of(step * span, span), span)], out_sems.at[slot]
        )

    def one_step(step, carry):
        slot = step % 2

        @pl.when(step >= 2)
        def _():
            drain(slot, step - 2).wait()

        if has_acc:
            fill(step).wait()
        for pair in range(STEP_COLS // 2):
            sides = []
            for side in range(2):
                col = step * STEP_COLS + 2 * pair + side
                sides.append(
                    jnp.concatenate(
                        [held[jnp.minimum(table_ref[r, col] + i * slots, empty)] for i, r in enumerate(row_ids)],
                        axis=0,
                    )
                )
            value = jnp.dot(x, jnp.concatenate(sides, axis=1), preferred_element_type=jnp.float32)
            where = slice(2 * pair * HD, 2 * (pair + 1) * HD)
            if has_acc:
                value = value + refs[5][step, :, where]
            stage[slot, :, where] = value.astype(out_ref.dtype)
        drain(slot, step).start()
        return carry

    lax.fori_loop(0, n_steps, one_step, 0)
    for step in range(max(0, n_steps - 2), n_steps):
        drain(step % 2, step).wait()


def projection(x, table, row_ids, sources, pieces, kept, acc, last):
    tokens, width = x.shape
    col_blocks = table.shape[1]
    n_rows = len(sources)
    slots = len(sources[0]) * kept
    shape = (tokens, col_blocks * HD)
    smem = pl.BlockSpec(memory_space=pltpu.SMEM)
    vmem = pl.BlockSpec(memory_space=pltpu.VMEM)
    hbm = pl.BlockSpec(memory_space=pl.ANY)
    scratch = [
        pltpu.VMEM((n_rows * slots + 1, HD, HD), jnp.bfloat16),
        pltpu.SemaphoreType.DMA((n_rows, len(sources[0]))),
    ]
    span = STEP_COLS * HD
    dtype = jnp.bfloat16 if last else jnp.float32
    scratch += [pltpu.VMEM((2, tokens, span), dtype), pltpu.SemaphoreType.DMA((2,))]
    if acc is not None:
        n_steps = col_blocks // STEP_COLS
        scratch += [pltpu.VMEM((n_steps, tokens, span), jnp.float32), pltpu.SemaphoreType.DMA((n_steps,))]
    return pl.pallas_call(
        functools.partial(projection_body, sources, kept, acc is not None),
        out_shape=pltpu.HBM(shape, dtype),
        in_specs=[smem, smem, vmem] + [hbm] * len(pieces) + ([hbm] if acc is not None else []),
        out_specs=hbm,
        scratch_shapes=scratch,
        compiler_params=pltpu.CompilerParams(vmem_limit_bytes=28 << 20),
        cost_estimate=pl.CostEstimate(flops=1, transcendentals=0, bytes_accessed=1),
        name="projection" if last else "early_projection",
    )(table, row_ids, x, in_hbm(pieces[0]), *pieces[1:], *(() if acc is None else (in_hbm(acc),)))


def swap(value, axis):
    return lax.ppermute(value, axis, [(0, 1), (1, 0)])


def after(value, *earlier):
    return lax.optimization_barrier((value,) + earlier)[0]


def peer_side(own):
    ck, sk, cv, sv = own
    return [swap(ck, "seq"), swap(jnp.concatenate([sk, sv], axis=0), "seq"), swap(cv, "seq")]


def column_table(all_columns, col_blocks):
    dp, _, kept = all_columns.shape
    slot = jnp.arange(dp, dtype=jnp.int32)[:, None] * kept + jnp.arange(kept, dtype=jnp.int32)[None, :]
    match = all_columns[..., None] == jnp.arange(col_blocks, dtype=jnp.int32)
    return jnp.min(jnp.where(match, slot[:, None, :, None], 1 << 20), axis=(0, 2))


def shards(mesh, queries, stretch_keys, stretch_values, cache_keys, cache_values, blocks, block_columns):
    width_dev = queries.shape[2]
    row_blocks, kept, block_size = blocks.shape[:3]
    col_blocks = mesh.shape["tensor"] * width_dev // block_size
    my_seq = lax.axis_index("seq")
    seq_one = my_seq.reshape(1)
    q = queries[0]
    own = [a[0] for a in (cache_keys, stretch_keys, cache_values, stretch_values)]
    flat = blocks.reshape(row_blocks * kept, block_size, block_size)

    if mesh.shape["dp"] == 2 and mesh.shape["groups"] == 2 and row_blocks % 16 == 0 and max(row_blocks, kept) <= block_size:
        unit = row_blocks // 16
        groups = lax.axis_index("groups")
        half = 8 * unit * my_seq
        relay = half + unit * (2 + 3 * groups)

        def piece(start, count, more=0):
            return lax.dynamic_slice_in_dim(flat, start * kept, count * kept + more, 0)

        heads = width_dev // (2 * HD)
        soon = max(heads // 4, 1)
        carried = jnp.pad(
            block_columns.astype(jnp.bfloat16), ((0, block_size - row_blocks), (0, block_size - kept))
        )
        near1 = swap(jnp.concatenate([piece(relay, unit), carried[None]], axis=0), "dp")
        near2 = swap(piece(relay + unit, 2 * unit), "dp")
        shared = swap(piece(half, 2 * unit, EXTRA), "dp")
        peer = peer_side(own)
        attended = attention(seq_one, q, own, peer, 0, soon)
        near1, attended = lax.optimization_barrier((near1, attended))
        peer_columns = near1[unit * kept, :row_blocks, :kept].astype(jnp.int32)
        table = column_table(jnp.stack([block_columns, peer_columns]), col_blocks)
        far1 = swap(near1[: unit * kept], "groups")
        near1_other = swap(near1[: unit * kept], "seq")
        attended = attention(seq_one, q, own, peer, soon, heads - soon, attended)
        near2, far1, attended = lax.optimization_barrier((near2, far1, attended))
        far2, far3 = [swap(near2[i * unit * kept : (i + 1) * unit * kept], "groups") for i in range(2)]
        near2_other = swap(near2, "seq")
        far1_other = swap(far1, "seq")
        other = 8 * unit * (1 - my_seq)

        def stage(plan, acc, last):
            row_list, sources, pieces = [], [], [flat]
            for start, count, value in plan:
                for i in range(count):
                    row_list.append(start + i)
                    sources.append(((0, 0, True), (len(pieces), i * kept, False)))
                pieces.append(value)
            return projection(attended, table, jnp.stack(row_list), tuple(sources), pieces, kept, acc, last)

        def relayed(base, group):
            return base + unit * (2 + 3 * group)

        early = stage(
            (
                (relayed(half, groups), unit, near1),
                (relayed(half, groups) + unit, 2 * unit, near2),
                (relayed(half, 1 - groups), unit, far1),
                (relayed(other, groups), unit, near1_other),
                (relayed(other, groups) + unit, 2 * unit, near2_other),
                (relayed(other, 1 - groups), unit, far1_other),
            ),
            None,
            False,
        )
        shared, far2, far3, early = lax.optimization_barrier((shared, far2, far3, early))
        shared_other = swap(shared[: 2 * unit * kept], "seq")
        far2_other = swap(far2, "seq")
        far3_other = swap(far3, "seq")
        partial_value = stage(
            (
                (half, 2 * unit, shared),
                (relayed(half, 1 - groups) + unit, unit, far2),
                (relayed(half, 1 - groups) + 2 * unit, unit, far3),
                (other, 2 * unit, shared_other),
                (relayed(other, 1 - groups) + unit, unit, far2_other),
                (relayed(other, 1 - groups) + 2 * unit, unit, far3_other),
            ),
            early,
            True,
        )
    else:
        dp = mesh.shape["dp"]
        gathered = lax.all_gather(flat, "dp", axis=0, tiled=True)
        table = column_table(lax.all_gather(block_columns, "dp", axis=0), col_blocks)
        peer = peer_side(own)
        attended = attention(seq_one, q, own, peer, 0, width_dev // (2 * HD))
        sources = tuple(tuple((0, d * row_blocks * kept, True) for d in range(dp)) for _ in range(row_blocks))
        partial_value = projection(
            attended, table, jnp.arange(row_blocks, dtype=jnp.int32), sources, [gathered], kept, None, True
        )
    owned = lax.psum_scatter(partial_value, "tensor", scatter_dimension=1, tiled=True)
    return owned[None]


def solution(mesh):
    token = P(("groups", "dp"), "seq", "tensor")
    placed = (token, token, token, token, token, P("tensor", "dp", None, None), P("tensor", "dp"))
    return jax.shard_map(
        functools.partial(shards, mesh),
        mesh=mesh,
        in_specs=placed,
        out_specs=token,
        check_vma=False,
    )
```

```python
import functools
import math

import jax
import jax.numpy as jnp
from jax import lax
from jax.experimental import pallas as pl
from jax.experimental.pallas import tpu as pltpu
from jax.sharding import PartitionSpec as P

HD = 128
FLOOR = -1e30
TILE = 768
STEP_COLS = 16
EXTRA = 3


def in_hbm(value):
    return pltpu.with_memory_space_constraint(value, pltpu.HBM)


def attention_body(seq_ref, q_ref, cka, ska, ckb, skb, cva, sva, cvb, svb, out_ref):
    rows = q_ref.shape[0]
    cache_rows = cka.shape[0]
    scale = HD ** (-0.5) * math.log2(math.e)
    q = q_ref[...].astype(jnp.float32) * scale
    q_hi = q.astype(jnp.bfloat16)
    q_lo = (q - q_hi.astype(jnp.float32)).astype(jnp.bfloat16)
    q_two = jnp.concatenate(
        [jnp.concatenate([q_hi[:, h * HD : (h + 1) * HD], q_lo[:, h * HD : (h + 1) * HD]], axis=1) for h in range(2)],
        axis=0,
    )
    whole = (cache_rows - 1) // TILE
    tiles = []
    for side, (ck, sk, cv, sv) in enumerate(((cka, ska, cva, sva), (ckb, skb, cvb, svb))):
        for t in range(whole):
            tiles.append((ck, cv, None, None, t * TILE, (t + 1) * TILE, None))
        tiles.append((ck, cv, sk, sv, whole * TILE, cache_rows, side))

    def take(main, fresh, lo, hi):
        return main[lo:hi, :] if fresh is None else jnp.concatenate([main[lo:hi, :], fresh[...]], axis=0)

    def score(tile):
        ck, _, sk, _, lo, hi, side = tile
        keys = take(ck, sk, lo, hi)
        scores = lax.dot_general(
            q_two,
            jnp.concatenate([keys, keys], axis=1),
            (((1,), (1,)), ((), ())),
            preferred_element_type=jnp.float32,
        )
        if side is None:
            return scores
        tail = scores[:, hi - lo :]
        if side == 0:
            token = lax.broadcasted_iota(jnp.int32, (rows, rows), 0)
            position = lax.broadcasted_iota(jnp.int32, (rows, rows), 1)
            seen = position <= token
            tail = jnp.where(jnp.concatenate([seen, seen], axis=0), tail, FLOOR)
        else:
            tail = jnp.where(seq_ref[0] > 0, tail, FLOOR)
        return jnp.concatenate([scores[:, : hi - lo], tail], axis=1)

    peak = acc = None
    upcoming = score(tiles[0])
    for i, tile in enumerate(tiles):
        scores = upcoming
        if i + 1 < len(tiles):
            upcoming = score(tiles[i + 1])
        tile_peak = jnp.max(scores, axis=1, keepdims=True)
        new_peak = tile_peak if peak is None else jnp.maximum(peak, tile_peak)
        expo = jnp.exp2(scores - new_peak).astype(jnp.bfloat16)
        values = take(tile[1], tile[3], tile[4], tile[5])
        added = jnp.dot(
            expo,
            jnp.concatenate([values, jnp.ones_like(values)], axis=1),
            preferred_element_type=jnp.float32,
        )
        acc = added if acc is None else acc * jnp.exp2(peak - new_peak) + added
        peak = new_peak
    result = acc[:, :HD] / acc[:, HD:]
    out_ref[:, :HD] = result[:rows].astype(out_ref.dtype)
    out_ref[:, HD:] = result[rows:].astype(out_ref.dtype)


def attention(my_seq, q, own, peer, first, count, earlier=None):
    rows, width = q.shape
    ck, sk, cv, sv = own
    pck, psk, pcv, psv = peer
    cache_rows = ck.shape[0]
    qspec = pl.BlockSpec((rows, 2 * HD), lambda g, s: (0, g + first))
    cspec = pl.BlockSpec((cache_rows, HD), lambda g, s: (0, g + first))
    nspec = pl.BlockSpec((rows, HD), lambda g, s: (0, g + first))
    args = [q, ck, sk, pck, psk, cv, sv, pcv, psv]
    specs = [qspec, cspec, nspec, cspec, nspec, cspec, nspec, cspec, nspec]
    body = attention_body
    aliases = {}
    if earlier is not None:
        body = lambda *refs: attention_body(*refs[:10], *refs[11:])
        args.append(earlier)
        specs.append(pl.BlockSpec(memory_space=pltpu.HBM))
        aliases = {10: 0}
    return pl.pallas_call(
        body,
        out_shape=pltpu.HBM((rows, width), jnp.bfloat16),
        grid_spec=pltpu.PrefetchScalarGridSpec(
            num_scalar_prefetch=1,
            grid=(count,),
            in_specs=specs,
            out_specs=qspec,
        ),
        input_output_aliases=aliases,
        compiler_params=pltpu.CompilerParams(
            dimension_semantics=("arbitrary",), vmem_limit_bytes=20 << 20
        ),
        cost_estimate=pl.CostEstimate(flops=1, transcendentals=0, bytes_accessed=1),
        name="attention" if earlier is None else "late_attention",
    )(my_seq, *[in_hbm(a) for a in args])


def projection_body(sources, kept, has_acc, table_ref, rows_ref, x_hbm, *refs):
    n_pieces = 1 + max(piece for row in sources for piece, _, _ in row)
    pieces = refs[:n_pieces]
    refs = refs[n_pieces:]
    if has_acc:
        acc_hbm, refs = refs[0], refs[1:]
    out_ref, held, sems, stage, out_sems, x_ref, x_sem = refs[:7]
    slots = len(sources[0]) * kept
    empty = len(sources) * slots
    row_ids = [rows_ref[i] for i in range(len(sources))]
    copies = []
    for i, row in enumerate(sources):
        for j, (piece, offset, by_row) in enumerate(row):
            start = offset + row_ids[i] * kept if by_row else offset
            copies.append(
                pltpu.make_async_copy(
                    pieces[piece].at[pl.ds(start, kept)],
                    held.at[pl.ds(i * slots + j * kept, kept)],
                    sems.at[i, j],
                )
            )
    x_copy = pltpu.make_async_copy(x_hbm, x_ref, x_sem)
    x_copy.start()
    for copy in copies:
        copy.start()
    n_steps = table_ref.shape[1] // STEP_COLS
    span = STEP_COLS * HD

    def fill(step):
        acc_ref, acc_sems = refs[7:]
        where = pl.ds(pl.multiple_of(step * span, span), span)
        return pltpu.make_async_copy(acc_hbm.at[:, where], acc_ref.at[step], acc_sems.at[step])

    if has_acc:
        for step in range(n_steps):
            fill(step).start()
    held[empty] = jnp.zeros(held.shape[1:], held.dtype)
    x_copy.wait()
    for copy in copies:
        copy.wait()
    x = jnp.concatenate([x_ref[:, pl.ds(pl.multiple_of(r * HD, HD), HD)] for r in row_ids], axis=1)

    def drain(slot, step):
        return pltpu.make_async_copy(
            stage.at[slot], out_ref.at[:, pl.ds(pl.multiple_of(step * span, span), span)], out_sems.at[slot]
        )

    def one_step(step, carry):
        slot = step % 2

        @pl.when(step >= 2)
        def _():
            drain(slot, step - 2).wait()

        if has_acc:
            fill(step).wait()
        for pair in range(STEP_COLS // 2):
            sides = []
            for side in range(2):
                col = step * STEP_COLS + 2 * pair + side
                sides.append(
                    jnp.concatenate(
                        [held[jnp.minimum(table_ref[r, col] + i * slots, empty)] for i, r in enumerate(row_ids)],
                        axis=0,
                    )
                )
            value = jnp.dot(x, jnp.concatenate(sides, axis=1), preferred_element_type=jnp.float32)
            where = slice(2 * pair * HD, 2 * (pair + 1) * HD)
            if has_acc:
                value = value + refs[7][step, :, where]
            stage[slot, :, where] = value.astype(out_ref.dtype)
        drain(slot, step).start()
        return carry

    lax.fori_loop(0, n_steps, one_step, 0)
    for step in range(max(0, n_steps - 2), n_steps):
        drain(step % 2, step).wait()


def projection(x, table, row_ids, sources, pieces, kept, acc, last):
    tokens, width = x.shape
    col_blocks = table.shape[1]
    n_rows = len(sources)
    slots = len(sources[0]) * kept
    shape = (tokens, col_blocks * HD)
    smem = pl.BlockSpec(memory_space=pltpu.SMEM)
    hbm = pl.BlockSpec(memory_space=pl.ANY)
    scratch = [
        pltpu.VMEM((n_rows * slots + 1, HD, HD), jnp.bfloat16),
        pltpu.SemaphoreType.DMA((n_rows, len(sources[0]))),
    ]
    span = STEP_COLS * HD
    dtype = jnp.bfloat16
    scratch += [pltpu.VMEM((2, tokens, span), dtype), pltpu.SemaphoreType.DMA((2,))]
    scratch += [pltpu.VMEM((tokens, width), x.dtype), pltpu.SemaphoreType.DMA(())]
    if acc is not None:
        n_steps = col_blocks // STEP_COLS
        scratch += [pltpu.VMEM((n_steps, tokens, span), dtype), pltpu.SemaphoreType.DMA((n_steps,))]
    return pl.pallas_call(
        functools.partial(projection_body, sources, kept, acc is not None),
        out_shape=pltpu.HBM(shape, dtype),
        in_specs=[smem, smem, hbm] + [hbm] * len(pieces) + ([hbm] if acc is not None else []),
        out_specs=hbm,
        scratch_shapes=scratch,
        compiler_params=pltpu.CompilerParams(vmem_limit_bytes=28 << 20),
        cost_estimate=pl.CostEstimate(flops=1, transcendentals=0, bytes_accessed=1),
        name="projection" if last else "early_projection",
    )(table, row_ids, in_hbm(x), in_hbm(pieces[0]), *[p if last else in_hbm(p) for p in pieces[1:]], *(() if acc is None else (in_hbm(acc),)))


def swap(value, axis):
    return lax.ppermute(value, axis, [(0, 1), (1, 0)])


def after(value, *earlier):
    return lax.optimization_barrier((value,) + earlier)[0]


def peer_side(own):
    ck, sk, cv, sv = own
    return [swap(a, "seq") for a in (ck, sk, cv, sv)]


def column_table(all_columns, col_blocks):
    dp, _, kept = all_columns.shape
    slot = jnp.arange(dp, dtype=jnp.int32)[:, None] * kept + jnp.arange(kept, dtype=jnp.int32)[None, :]
    match = all_columns[..., None] == jnp.arange(col_blocks, dtype=jnp.int32)
    return jnp.min(jnp.where(match, slot[:, None, :, None], 1 << 20), axis=(0, 2))


def shards(mesh, queries, stretch_keys, stretch_values, cache_keys, cache_values, blocks, block_columns):
    width_dev = queries.shape[2]
    row_blocks, kept, block_size = blocks.shape[:3]
    col_blocks = mesh.shape["tensor"] * width_dev // block_size
    my_seq = lax.axis_index("seq")
    seq_one = my_seq.reshape(1)
    q = queries[0]
    own = [a[0] for a in (cache_keys, stretch_keys, cache_values, stretch_values)]
    flat = blocks.reshape(row_blocks * kept, block_size, block_size)

    if mesh.shape["dp"] == 2 and mesh.shape["groups"] == 2 and row_blocks % 16 == 0 and max(row_blocks, kept) <= block_size:
        unit = row_blocks // 16
        groups = lax.axis_index("groups")
        half = 8 * unit * my_seq
        relay = half + unit * (2 + 3 * groups)

        def piece(start, count, more=0):
            return lax.dynamic_slice_in_dim(flat, start * kept, count * kept + more, 0)

        heads = width_dev // (2 * HD)
        soon = max(heads // 4, 1)
        carried = jnp.pad(
            block_columns.astype(jnp.bfloat16), ((0, block_size - row_blocks), (0, block_size - kept))
        )
        near1 = swap(jnp.concatenate([piece(relay, unit), carried[None]], axis=0), "dp")
        near2 = swap(piece(relay + unit, 2 * unit), "dp")
        peer = peer_side(own)
        shared, peer[0] = lax.optimization_barrier((piece(half, 2 * unit, EXTRA), peer[0]))
        shared = swap(shared, "dp")
        attended = attention(seq_one, q, own, peer, 0, soon)
        near1, attended = lax.optimization_barrier((near1, attended))
        peer_columns = near1[unit * kept, :row_blocks, :kept].astype(jnp.int32)
        table = column_table(jnp.stack([block_columns, peer_columns]), col_blocks)
        far1 = swap(near1, "groups")
        near1_other = swap(near1, "seq")
        attended = attention(seq_one, q, own, peer, soon, heads - 2 * soon, attended)
        near2, far1, attended = lax.optimization_barrier((near2, far1, attended))
        far2, far3 = [swap(near2[i * unit * kept : (i + 1) * unit * kept], "groups") for i in range(2)]
        near2_other = swap(near2, "seq")
        far1_other = swap(far1, "seq")
        attended = attention(seq_one, q, own, peer, heads - soon, soon, attended)
        other = 8 * unit * (1 - my_seq)

        def stage(plan, acc, last):
            row_list, sources, pieces = [], [], [flat]
            for start, count, value in plan:
                for i in range(count):
                    row_list.append(start + i)
                    sources.append(((0, 0, True), (len(pieces), i * kept, False)))
                pieces.append(value)
            return projection(attended, table, jnp.stack(row_list), tuple(sources), pieces, kept, acc, last)

        def relayed(base, group):
            return base + unit * (2 + 3 * group)

        early = stage(
            (
                (relayed(half, groups), unit, near1),
                (relayed(half, groups) + unit, 2 * unit, near2),
                (relayed(half, 1 - groups), unit, far1),
                (relayed(other, groups), unit, near1_other),
                (relayed(other, groups) + unit, 2 * unit, near2_other),
                (relayed(other, 1 - groups), unit, far1_other),
            ),
            None,
            False,
        )
        shared, far2, far3, early = lax.optimization_barrier((shared, far2, far3, early))
        shared_other = swap(shared, "seq")
        far2_other = swap(far2, "seq")
        far3_other = swap(far3, "seq")
        partial_value = stage(
            (
                (half, 2 * unit, shared),
                (relayed(half, 1 - groups) + unit, unit, far2),
                (relayed(half, 1 - groups) + 2 * unit, unit, far3),
                (other, 2 * unit, shared_other),
                (relayed(other, 1 - groups) + unit, unit, far2_other),
                (relayed(other, 1 - groups) + 2 * unit, unit, far3_other),
            ),
            early,
            True,
        )
    else:
        dp = mesh.shape["dp"]
        gathered = lax.all_gather(flat, "dp", axis=0, tiled=True)
        table = column_table(lax.all_gather(block_columns, "dp", axis=0), col_blocks)
        peer = peer_side(own)
        attended = attention(seq_one, q, own, peer, 0, width_dev // (2 * HD))
        sources = tuple(tuple((0, d * row_blocks * kept, True) for d in range(dp)) for _ in range(row_blocks))
        partial_value = projection(
            attended, table, jnp.arange(row_blocks, dtype=jnp.int32), sources, [gathered], kept, None, True
        )
    owned = lax.psum_scatter(partial_value, "tensor", scatter_dimension=1, tiled=True)
    return owned[None]


def solution(mesh):
    token = P(("groups", "dp"), "seq", "tensor")
    placed = (token, token, token, token, token, P("tensor", "dp", None, None), P("tensor", "dp"))
    return jax.shard_map(
        functools.partial(shards, mesh),
        mesh=mesh,
        in_specs=placed,
        out_specs=token,
        check_vma=False,
    )
```

```python
import functools
import math

import jax
import jax.numpy as jnp
from jax import lax
from jax.experimental import pallas as pl
from jax.experimental.pallas import tpu as pltpu
from jax.sharding import PartitionSpec as P

HD = 128
FLOOR = -1e30
TILE = 768
STEP_COLS = 16
EXTRA = 3


def in_hbm(value):
    return pltpu.with_memory_space_constraint(value, pltpu.HBM)


def attention_body(seq_ref, q_ref, cka, ska, ckb, skb, cva, sva, cvb, svb, out_ref):
    rows = q_ref.shape[0]
    cache_rows = cka.shape[0]
    scale = HD ** (-0.5) * math.log2(math.e)
    q = q_ref[...].astype(jnp.float32) * scale
    q_hi = q.astype(jnp.bfloat16)
    q_lo = (q - q_hi.astype(jnp.float32)).astype(jnp.bfloat16)
    q_two = jnp.concatenate(
        [jnp.concatenate([q_hi[:, h * HD : (h + 1) * HD], q_lo[:, h * HD : (h + 1) * HD]], axis=1) for h in range(2)],
        axis=0,
    )
    whole = (cache_rows - 1) // TILE
    tiles = []
    for side, (ck, sk, cv, sv) in enumerate(((cka, ska, cva, sva), (ckb, skb, cvb, svb))):
        for t in range(whole):
            tiles.append((ck, cv, None, None, t * TILE, (t + 1) * TILE, None))
        tiles.append((ck, cv, sk, sv, whole * TILE, cache_rows, side))

    def take(main, fresh, lo, hi):
        return main[lo:hi, :] if fresh is None else jnp.concatenate([main[lo:hi, :], fresh[...]], axis=0)

    def score(tile):
        ck, _, sk, _, lo, hi, side = tile
        keys = take(ck, sk, lo, hi)
        scores = lax.dot_general(
            q_two,
            jnp.concatenate([keys, keys], axis=1),
            (((1,), (1,)), ((), ())),
            preferred_element_type=jnp.float32,
        )
        if side is None:
            return scores
        tail = scores[:, hi - lo :]
        if side == 0:
            token = lax.broadcasted_iota(jnp.int32, (rows, rows), 0)
            position = lax.broadcasted_iota(jnp.int32, (rows, rows), 1)
            seen = position <= token
            tail = jnp.where(jnp.concatenate([seen, seen], axis=0), tail, FLOOR)
        else:
            tail = jnp.where(seq_ref[0] > 0, tail, FLOOR)
        return jnp.concatenate([scores[:, : hi - lo], tail], axis=1)

    peak = acc = None
    upcoming = score(tiles[0])
    for i, tile in enumerate(tiles):
        scores = upcoming
        if i + 1 < len(tiles):
            upcoming = score(tiles[i + 1])
        tile_peak = jnp.max(scores, axis=1, keepdims=True)
        new_peak = tile_peak if peak is None else jnp.maximum(peak, tile_peak)
        expo = jnp.exp2(scores - new_peak).astype(jnp.bfloat16)
        values = take(tile[1], tile[3], tile[4], tile[5])
        added = jnp.dot(
            expo,
            jnp.concatenate([values, jnp.ones_like(values)], axis=1),
            preferred_element_type=jnp.float32,
        )
        acc = added if acc is None else acc * jnp.exp2(peak - new_peak) + added
        peak = new_peak
    result = acc[:, :HD] / acc[:, HD:]
    out_ref[:, :HD] = result[:rows].astype(out_ref.dtype)
    out_ref[:, HD:] = result[rows:].astype(out_ref.dtype)


def attention(my_seq, q, own, peer, first, count, earlier=None):
    rows, width = q.shape
    ck, sk, cv, sv = own
    pck, psk, pcv, psv = peer
    cache_rows = ck.shape[0]
    qspec = pl.BlockSpec((rows, 2 * HD), lambda g, s: (0, g + first))
    cspec = pl.BlockSpec((cache_rows, HD), lambda g, s: (0, g + first))
    nspec = pl.BlockSpec((rows, HD), lambda g, s: (0, g + first))
    args = [q, ck, sk, pck, psk, cv, sv, pcv, psv]
    specs = [qspec, cspec, nspec, cspec, nspec, cspec, nspec, cspec, nspec]
    body = attention_body
    aliases = {}
    if earlier is not None:
        body = lambda *refs: attention_body(*refs[:10], *refs[11:])
        args.append(earlier)
        specs.append(pl.BlockSpec(memory_space=pltpu.HBM))
        aliases = {10: 0}
    return pl.pallas_call(
        body,
        out_shape=pltpu.HBM((rows, width), jnp.bfloat16),
        grid_spec=pltpu.PrefetchScalarGridSpec(
            num_scalar_prefetch=1,
            grid=(count,),
            in_specs=specs,
            out_specs=qspec,
        ),
        input_output_aliases=aliases,
        compiler_params=pltpu.CompilerParams(
            dimension_semantics=("arbitrary",), vmem_limit_bytes=20 << 20
        ),
        cost_estimate=pl.CostEstimate(flops=1, transcendentals=0, bytes_accessed=1),
        name="attention" if earlier is None else "late_attention",
    )(my_seq, *[in_hbm(a) for a in args])


def projection_body(sources, kept, has_acc, split, n_steps, table_ref, rows_ref, cols_ref, x_hbm, *refs):
    n_pieces = 1 + max(piece for row in sources for piece, _, _ in row)
    pieces, refs = refs[:n_pieces], refs[n_pieces:]
    if has_acc:
        acc_hbm, refs = refs[0], refs[1:]
    n_outs = 2 * n_steps if split else 1
    outs, refs = refs[:n_outs], refs[n_outs:]
    held, sems, stage, out_sems, x_ref, x_sem = refs[:6]
    slots = len(sources[0]) * kept
    empty = len(sources) * slots
    row_ids = [rows_ref[i] for i in range(len(sources))]
    step_cols = stage.shape[2] // HD
    span = step_cols * HD
    tokens = stage.shape[1]
    copies = [pltpu.make_async_copy(x_hbm, x_ref, x_sem)]
    for i, row in enumerate(sources):
        for j, (piece, offset, by_row) in enumerate(row):
            start = offset + row_ids[i] * kept if by_row else offset
            copies.append(
                pltpu.make_async_copy(
                    pieces[piece].at[pl.ds(start, kept)],
                    held.at[pl.ds(i * slots + j * kept, kept)],
                    sems.at[i, j],
                )
            )
    for copy in copies:
        copy.start()
    where = [pl.ds(pl.multiple_of(cols_ref[step] * HD, span), span) for step in range(n_steps)]
    fills = []
    if has_acc:
        acc_ref, acc_sems = refs[6:]
        for step in range(n_steps):
            fills.append(pltpu.make_async_copy(acc_hbm.at[:, where[step]], acc_ref.at[step], acc_sems.at[step]))
            fills[step].start()
    held[empty] = jnp.zeros(held.shape[1:], held.dtype)
    for copy in copies:
        copy.wait()
    x = jnp.concatenate([x_ref[:, pl.ds(pl.multiple_of(r * HD, HD), HD)] for r in row_ids], axis=1)
    drains = []
    for step in range(n_steps):
        slot = step % 2
        if split:
            half = tokens // 2
            drains.append(
                [
                    pltpu.make_async_copy(
                        stage.at[slot, pl.ds(side * half, half)], outs[2 * step + side], out_sems.at[slot, side]
                    )
                    for side in range(2)
                ]
            )
        else:
            drains.append([pltpu.make_async_copy(stage.at[slot], outs[0].at[:, where[step]], out_sems.at[slot, 0])])
        if step >= 2:
            for copy in drains[step - 2]:
                copy.wait()
        if has_acc:
            fills[step].wait()
        for pair in range(step_cols // 2):
            sides = []
            for side in range(2):
                col = cols_ref[step] + 2 * pair + side
                sides.append(
                    jnp.concatenate(
                        [held[jnp.minimum(table_ref[r, col] + i * slots, empty)] for i, r in enumerate(row_ids)],
                        axis=0,
                    )
                )
            value = jnp.dot(x, jnp.concatenate(sides, axis=1), preferred_element_type=jnp.float32)
            lanes = slice(2 * pair * HD, 2 * (pair + 1) * HD)
            if has_acc:
                value = value + acc_ref[step, :, lanes]
            stage[slot, :, lanes] = value.astype(stage.dtype)
        for copy in drains[step]:
            copy.start()
    for step in range(max(0, n_steps - 2), n_steps):
        for copy in drains[step]:
            copy.wait()


def projection(x, table, row_ids, sources, pieces, kept, acc=None, columns=None):
    tokens, width = x.shape
    col_blocks = table.shape[1]
    n_rows = len(sources)
    slots = len(sources[0]) * kept
    split = columns is not None
    if split:
        step_cols, n_steps = width // HD, columns.shape[0]
        out_shape = [pltpu.HBM((tokens // 2, width), x.dtype)] * (2 * n_steps)
    else:
        step_cols = min(STEP_COLS, col_blocks)
        n_steps = col_blocks // step_cols
        columns = jnp.arange(n_steps, dtype=jnp.int32) * step_cols
        out_shape = [pltpu.HBM((tokens, col_blocks * HD), x.dtype)]
    span = step_cols * HD
    smem = pl.BlockSpec(memory_space=pltpu.SMEM)
    hbm = pl.BlockSpec(memory_space=pl.ANY)
    scratch = [
        pltpu.VMEM((n_rows * slots + 1, HD, HD), x.dtype),
        pltpu.SemaphoreType.DMA((n_rows, len(sources[0]))),
        pltpu.VMEM((2, tokens, span), x.dtype),
        pltpu.SemaphoreType.DMA((2, 2)),
        pltpu.VMEM((tokens, width), x.dtype),
        pltpu.SemaphoreType.DMA(()),
    ]
    if acc is not None:
        scratch += [pltpu.VMEM((n_steps, tokens, span), x.dtype), pltpu.SemaphoreType.DMA((n_steps,))]
    return pl.pallas_call(
        functools.partial(projection_body, sources, kept, acc is not None, split, n_steps),
        out_shape=out_shape,
        in_specs=[smem, smem, smem, hbm] + [hbm] * len(pieces) + ([hbm] if acc is not None else []),
        out_specs=[hbm] * len(out_shape),
        scratch_shapes=scratch,
        compiler_params=pltpu.CompilerParams(vmem_limit_bytes=28 << 20),
        cost_estimate=pl.CostEstimate(flops=1, transcendentals=0, bytes_accessed=1),
        name="projection" if split else "early_projection",
    )(
        table,
        row_ids,
        columns,
        in_hbm(x),
        in_hbm(pieces[0]),
        *[p if split else in_hbm(p) for p in pieces[1:]],
        *(() if acc is None else (in_hbm(acc),)),
    )


def add(*values):
    return sum(v.astype(jnp.float32) for v in values).astype(values[0].dtype)


def line_scatter(parts, n):
    arrived = [None, None]
    for step in range(1, n):
        for half in range(2):
            up, down = parts(n - step)[half], parts(step)[half]
            if arrived[half] is not None:
                from_below, from_above = lax.optimization_barrier(arrived[half])
                up, down = add(up, from_below), add(down, from_above)
            arrived[half] = (
                lax.ppermute(up, "tensor", [(i, i + 1) for i in range(step)]),
                lax.ppermute(down, "tensor", [(i + 1, i) for i in range(n - 1 - step, n - 1)]),
            )
    return jnp.concatenate([add(parts(0)[half], *arrived[half]) for half in range(2)], axis=0)


def swap(value, axis):
    return lax.ppermute(value, axis, [(0, 1), (1, 0)])


def after(value, *earlier):
    return lax.optimization_barrier((value,) + earlier)[0]


def peer_side(own):
    ck, sk, cv, sv = own
    return [swap(a, "seq") for a in (ck, sk, cv, sv)]


def column_table(all_columns, col_blocks):
    dp, _, kept = all_columns.shape
    slot = jnp.arange(dp, dtype=jnp.int32)[:, None] * kept + jnp.arange(kept, dtype=jnp.int32)[None, :]
    match = all_columns[..., None] == jnp.arange(col_blocks, dtype=jnp.int32)
    return jnp.min(jnp.where(match, slot[:, None, :, None], 1 << 20), axis=(0, 2))


def shards(mesh, queries, stretch_keys, stretch_values, cache_keys, cache_values, blocks, block_columns):
    width_dev = queries.shape[2]
    row_blocks, kept, block_size = blocks.shape[:3]
    col_blocks = mesh.shape["tensor"] * width_dev // block_size
    my_seq = lax.axis_index("seq")
    seq_one = my_seq.reshape(1)
    q = queries[0]
    own = [a[0] for a in (cache_keys, stretch_keys, cache_values, stretch_values)]
    flat = blocks.reshape(row_blocks * kept, block_size, block_size)

    if mesh.shape["dp"] == 2 and mesh.shape["groups"] == 2 and row_blocks % 16 == 0 and max(row_blocks, kept) <= block_size:
        unit = row_blocks // 16
        groups = lax.axis_index("groups")
        half = 8 * unit * my_seq
        relay = half + unit * (2 + 3 * groups)

        def piece(start, count, more=0):
            return lax.dynamic_slice_in_dim(flat, start * kept, count * kept + more, 0)

        heads = width_dev // (2 * HD)
        soon = max(heads // 4, 1)
        carried = jnp.pad(
            block_columns.astype(jnp.bfloat16), ((0, block_size - row_blocks), (0, block_size - kept))
        )
        near1 = swap(jnp.concatenate([piece(relay, unit), carried[None]], axis=0), "dp")
        near2 = swap(piece(relay + unit, 2 * unit), "dp")
        peer = peer_side(own)
        shared, peer[0] = lax.optimization_barrier((piece(half, 2 * unit, EXTRA), peer[0]))
        shared = swap(shared, "dp")
        attended = attention(seq_one, q, own, peer, 0, soon)
        near1, attended = lax.optimization_barrier((near1, attended))
        peer_columns = near1[unit * kept, :row_blocks, :kept].astype(jnp.int32)
        table = column_table(jnp.stack([block_columns, peer_columns]), col_blocks)
        far1 = swap(near1, "groups")
        near1_other = swap(near1, "seq")
        attended = attention(seq_one, q, own, peer, soon, heads - 2 * soon, attended)
        near2, far1, attended = lax.optimization_barrier((near2, far1, attended))
        far2, far3 = [swap(near2[i * unit * kept : (i + 1) * unit * kept], "groups") for i in range(2)]
        near2_other = swap(near2, "seq")
        far1_other = swap(far1, "seq")
        attended = attention(seq_one, q, own, peer, heads - soon, soon, attended)
        other = 8 * unit * (1 - my_seq)

        def stage(plan, acc=None, columns=None):
            row_list, sources, pieces = [], [], [flat]
            for start, count, value in plan:
                for i in range(count):
                    row_list.append(start + i)
                    sources.append(((0, 0, True), (len(pieces), i * kept, False)))
                pieces.append(value)
            return projection(attended, table, jnp.stack(row_list), tuple(sources), pieces, kept, acc, columns)

        def relayed(base, group):
            return base + unit * (2 + 3 * group)

        (early,) = stage(
            (
                (relayed(half, groups), unit, near1),
                (relayed(half, groups) + unit, 2 * unit, near2),
                (relayed(half, 1 - groups), unit, far1),
                (relayed(other, groups), unit, near1_other),
                (relayed(other, groups) + unit, 2 * unit, near2_other),
                (relayed(other, 1 - groups), unit, far1_other),
            ),
        )
        shared, far2, far3, early = lax.optimization_barrier((shared, far2, far3, early))
        shared_other = swap(shared, "seq")
        far2_other = swap(far2, "seq")
        far3_other = swap(far3, "seq")
        plan = (
            (half, 2 * unit, shared),
            (relayed(half, 1 - groups) + unit, unit, far2),
            (relayed(half, 1 - groups) + 2 * unit, unit, far3),
            (other, 2 * unit, shared_other),
            (relayed(other, 1 - groups) + unit, unit, far2_other),
            (relayed(other, 1 - groups) + 2 * unit, unit, far3_other),
        )
        n = mesh.shape["tensor"]
        place = lax.axis_index("tensor")
        sums = {}
        for group in (sorted({n - 1, 1}), sorted(set(range(n)) - {n - 1, 1})):
            if group:
                columns = jnp.stack([(place + j) % n * row_blocks for j in group])
                found = stage(plan, early, columns)
                for i, j in enumerate(group):
                    sums[j] = found[2 * i : 2 * i + 2]
        return line_scatter(lambda j: sums[j], n)[None]
    else:
        dp = mesh.shape["dp"]
        gathered = lax.all_gather(flat, "dp", axis=0, tiled=True)
        table = column_table(lax.all_gather(block_columns, "dp", axis=0), col_blocks)
        peer = peer_side(own)
        attended = attention(seq_one, q, own, peer, 0, width_dev // (2 * HD))
        sources = tuple(tuple((0, d * row_blocks * kept, True) for d in range(dp)) for _ in range(row_blocks))
        (partial_value,) = projection(
            attended, table, jnp.arange(row_blocks, dtype=jnp.int32), sources, [gathered], kept
        )
    owned = lax.psum_scatter(partial_value, "tensor", scatter_dimension=1, tiled=True)
    return owned[None]


def solution(mesh):
    token = P(("groups", "dp"), "seq", "tensor")
    placed = (token, token, token, token, token, P("tensor", "dp", None, None), P("tensor", "dp"))
    return jax.shard_map(
        functools.partial(shards, mesh),
        mesh=mesh,
        in_specs=placed,
        out_specs=token,
        check_vma=False,
    )
```

```python
import functools
import math

import jax
import jax.numpy as jnp
from jax import lax
from jax.experimental import pallas as pl
from jax.experimental.pallas import tpu as pltpu
from jax.sharding import PartitionSpec as P

HD = 128
FLOOR = -1e30
TILE = 768
STEP_COLS = 16
EXTRA = 3


def in_hbm(value):
    return pltpu.with_memory_space_constraint(value, pltpu.HBM)


def attention_body(seq_ref, q_ref, cka, ska, ckb, skb, cva, sva, cvb, svb, out_ref):
    rows = q_ref.shape[0]
    cache_rows = cka.shape[0]
    scale = HD ** (-0.5) * math.log2(math.e)
    q = q_ref[...].astype(jnp.float32) * scale
    q_hi = q.astype(jnp.bfloat16)
    q_lo = (q - q_hi.astype(jnp.float32)).astype(jnp.bfloat16)
    q_two = jnp.concatenate(
        [jnp.concatenate([q_hi[:, h * HD : (h + 1) * HD], q_lo[:, h * HD : (h + 1) * HD]], axis=1) for h in range(2)],
        axis=0,
    )
    whole = (cache_rows - 1) // TILE
    tiles = []
    for side, (ck, sk, cv, sv) in enumerate(((cka, ska, cva, sva), (ckb, skb, cvb, svb))):
        for t in range(whole):
            tiles.append((ck, cv, None, None, t * TILE, (t + 1) * TILE, None))
        tiles.append((ck, cv, sk, sv, whole * TILE, cache_rows, side))

    def take(main, fresh, lo, hi):
        return main[lo:hi, :] if fresh is None else jnp.concatenate([main[lo:hi, :], fresh[...]], axis=0)

    def score(tile):
        ck, _, sk, _, lo, hi, side = tile
        keys = take(ck, sk, lo, hi)
        scores = lax.dot_general(
            q_two,
            jnp.concatenate([keys, keys], axis=1),
            (((1,), (1,)), ((), ())),
            preferred_element_type=jnp.float32,
        )
        if side is None:
            return scores
        tail = scores[:, hi - lo :]
        if side == 0:
            token = lax.broadcasted_iota(jnp.int32, (rows, rows), 0)
            position = lax.broadcasted_iota(jnp.int32, (rows, rows), 1)
            seen = position <= token
            tail = jnp.where(jnp.concatenate([seen, seen], axis=0), tail, FLOOR)
        else:
            tail = jnp.where(seq_ref[0] > 0, tail, FLOOR)
        return jnp.concatenate([scores[:, : hi - lo], tail], axis=1)

    peak = acc = None
    upcoming = score(tiles[0])
    for i, tile in enumerate(tiles):
        scores = upcoming
        if i + 1 < len(tiles):
            upcoming = score(tiles[i + 1])
        tile_peak = jnp.max(scores, axis=1, keepdims=True)
        new_peak = tile_peak if peak is None else jnp.maximum(peak, tile_peak)
        expo = jnp.exp2(scores - new_peak).astype(jnp.bfloat16)
        values = take(tile[1], tile[3], tile[4], tile[5])
        added = jnp.dot(
            expo,
            jnp.concatenate([values, jnp.ones_like(values)], axis=1),
            preferred_element_type=jnp.float32,
        )
        acc = added if acc is None else acc * jnp.exp2(peak - new_peak) + added
        peak = new_peak
    result = acc[:, :HD] / acc[:, HD:]
    out_ref[:, :HD] = result[:rows].astype(out_ref.dtype)
    out_ref[:, HD:] = result[rows:].astype(out_ref.dtype)


def attention(my_seq, q, own, peer, first, count, earlier=None):
    rows, width = q.shape
    ck, sk, cv, sv = own
    pck, psk, pcv, psv = peer
    cache_rows = ck.shape[0]
    qspec = pl.BlockSpec((rows, 2 * HD), lambda g, s: (0, g + first))
    cspec = pl.BlockSpec((cache_rows, HD), lambda g, s: (0, g + first))
    nspec = pl.BlockSpec((rows, HD), lambda g, s: (0, g + first))
    args = [q, ck, sk, pck, psk, cv, sv, pcv, psv]
    specs = [qspec, cspec, nspec, cspec, nspec, cspec, nspec, cspec, nspec]
    body = attention_body
    aliases = {}
    if earlier is not None:
        body = lambda *refs: attention_body(*refs[:10], *refs[11:])
        args.append(earlier)
        specs.append(pl.BlockSpec(memory_space=pltpu.HBM))
        aliases = {10: 0}
    return pl.pallas_call(
        body,
        out_shape=pltpu.HBM((rows, width), jnp.bfloat16),
        grid_spec=pltpu.PrefetchScalarGridSpec(
            num_scalar_prefetch=1,
            grid=(count,),
            in_specs=specs,
            out_specs=qspec,
        ),
        input_output_aliases=aliases,
        compiler_params=pltpu.CompilerParams(
            dimension_semantics=("arbitrary",), vmem_limit_bytes=20 << 20
        ),
        cost_estimate=pl.CostEstimate(flops=1, transcendentals=0, bytes_accessed=1),
        name="attention" if earlier is None else "late_attention",
    )(my_seq, *[in_hbm(a) for a in args])


def projection_body(sources, kept, has_acc, split, n_steps, table_ref, rows_ref, cols_ref, x_hbm, *refs):
    n_pieces = 1 + max(piece for row in sources for piece, _, _ in row)
    pieces, refs = refs[:n_pieces], refs[n_pieces:]
    if has_acc:
        acc_hbm, refs = refs[0], refs[1:]
    n_outs = 2 * n_steps if split else 1
    outs, refs = refs[:n_outs], refs[n_outs:]
    held, sems, stage, out_sems, x_ref, x_sem = refs[:6]
    slots = len(sources[0]) * kept
    empty = len(sources) * slots
    row_ids = [rows_ref[i] for i in range(len(sources))]
    step_cols = stage.shape[2] // HD
    span = step_cols * HD
    tokens = stage.shape[1]
    copies = [pltpu.make_async_copy(x_hbm, x_ref, x_sem)]
    for i, row in enumerate(sources):
        for j, (piece, offset, by_row) in enumerate(row):
            start = offset + row_ids[i] * kept if by_row else offset
            copies.append(
                pltpu.make_async_copy(
                    pieces[piece].at[pl.ds(start, kept)],
                    held.at[pl.ds(i * slots + j * kept, kept)],
                    sems.at[i, j],
                )
            )
    for copy in copies:
        copy.start()
    where = [pl.ds(pl.multiple_of(cols_ref[step] * HD, span), span) for step in range(n_steps)]
    fills = []
    if has_acc:
        acc_ref, acc_sems = refs[6:]
        for step in range(n_steps):
            fills.append(pltpu.make_async_copy(acc_hbm.at[:, where[step]], acc_ref.at[step], acc_sems.at[step]))
            fills[step].start()
    held[empty] = jnp.zeros(held.shape[1:], held.dtype)
    for copy in copies:
        copy.wait()
    x = jnp.concatenate([x_ref[:, pl.ds(pl.multiple_of(r * HD, HD), HD)] for r in row_ids], axis=1)
    drains = []
    for step in range(n_steps):
        slot = step % 2
        if split:
            half = tokens // 2
            drains.append(
                [
                    pltpu.make_async_copy(
                        stage.at[slot, pl.ds(side * half, half)], outs[2 * step + side], out_sems.at[slot, side]
                    )
                    for side in range(2)
                ]
            )
        else:
            drains.append([pltpu.make_async_copy(stage.at[slot], outs[0].at[:, where[step]], out_sems.at[slot, 0])])
        if step >= 2:
            for copy in drains[step - 2]:
                copy.wait()
        if has_acc:
            fills[step].wait()
        for pair in range(step_cols // 2):
            sides = []
            for side in range(2):
                col = cols_ref[step] + 2 * pair + side
                sides.append(
                    jnp.concatenate(
                        [held[jnp.minimum(table_ref[r, col] + i * slots, empty)] for i, r in enumerate(row_ids)],
                        axis=0,
                    )
                )
            value = jnp.dot(x, jnp.concatenate(sides, axis=1), preferred_element_type=jnp.float32)
            lanes = slice(2 * pair * HD, 2 * (pair + 1) * HD)
            if has_acc:
                value = value + acc_ref[step, :, lanes]
            stage[slot, :, lanes] = value.astype(stage.dtype)
        for copy in drains[step]:
            copy.start()
    for step in range(max(0, n_steps - 2), n_steps):
        for copy in drains[step]:
            copy.wait()


def projection(x, table, row_ids, sources, pieces, kept, acc=None, columns=None):
    tokens, width = x.shape
    col_blocks = table.shape[1]
    n_rows = len(sources)
    slots = len(sources[0]) * kept
    split = columns is not None
    if split:
        step_cols, n_steps = width // HD, columns.shape[0]
        out_shape = [pltpu.HBM((tokens // 2, width), x.dtype)] * (2 * n_steps)
    else:
        step_cols = min(STEP_COLS, col_blocks)
        n_steps = col_blocks // step_cols
        columns = jnp.arange(n_steps, dtype=jnp.int32) * step_cols
        out_shape = [pltpu.HBM((tokens, col_blocks * HD), x.dtype)]
    span = step_cols * HD
    smem = pl.BlockSpec(memory_space=pltpu.SMEM)
    hbm = pl.BlockSpec(memory_space=pl.ANY)
    scratch = [
        pltpu.VMEM((n_rows * slots + 1, HD, HD), x.dtype),
        pltpu.SemaphoreType.DMA((n_rows, len(sources[0]))),
        pltpu.VMEM((2, tokens, span), x.dtype),
        pltpu.SemaphoreType.DMA((2, 2)),
        pltpu.VMEM((tokens, width), x.dtype),
        pltpu.SemaphoreType.DMA(()),
    ]
    if acc is not None:
        scratch += [pltpu.VMEM((n_steps, tokens, span), x.dtype), pltpu.SemaphoreType.DMA((n_steps,))]
    return pl.pallas_call(
        functools.partial(projection_body, sources, kept, acc is not None, split, n_steps),
        out_shape=out_shape,
        in_specs=[smem, smem, smem, hbm] + [hbm] * len(pieces) + ([hbm] if acc is not None else []),
        out_specs=[hbm] * len(out_shape),
        scratch_shapes=scratch,
        compiler_params=pltpu.CompilerParams(vmem_limit_bytes=28 << 20),
        cost_estimate=pl.CostEstimate(flops=1, transcendentals=0, bytes_accessed=1),
        name="projection" if split else "early_projection",
    )(
        table,
        row_ids,
        columns,
        in_hbm(x),
        in_hbm(pieces[0]),
        *[p if split else in_hbm(p) for p in pieces[1:]],
        *(() if acc is None else (in_hbm(acc),)),
    )


def add(*values):
    return sum(v.astype(jnp.float32) for v in values).astype(values[0].dtype)


def line_scatter(parts, n):
    arrived = [None, None]
    for step in range(1, n):
        for half in range(2):
            up, down = parts(n - step)[half], parts(step)[half]
            if arrived[half] is not None:
                from_below, from_above = lax.optimization_barrier(arrived[half])
                up, down = add(up, from_below), add(down, from_above)
            arrived[half] = (
                lax.ppermute(up, "tensor", [(i, i + 1) for i in range(step)]),
                lax.ppermute(down, "tensor", [(i + 1, i) for i in range(n - 1 - step, n - 1)]),
            )
    return jnp.concatenate([add(parts(0)[half], *arrived[half]) for half in range(2)], axis=0)


def swap(value, axis):
    return lax.ppermute(value, axis, [(0, 1), (1, 0)])


def after(value, *earlier):
    return lax.optimization_barrier((value,) + earlier)[0]


def peer_side(own):
    ck, sk, cv, sv = own
    return [swap(a, "seq") for a in (ck, sk, cv, sv)]


def column_table(all_columns, col_blocks):
    dp, _, kept = all_columns.shape
    slot = jnp.arange(dp, dtype=jnp.int32)[:, None] * kept + jnp.arange(kept, dtype=jnp.int32)[None, :]
    match = all_columns[..., None] == jnp.arange(col_blocks, dtype=jnp.int32)
    return jnp.min(jnp.where(match, slot[:, None, :, None], 1 << 20), axis=(0, 2))


def shards(mesh, queries, stretch_keys, stretch_values, cache_keys, cache_values, blocks, block_columns):
    width_dev = queries.shape[2]
    row_blocks, kept, block_size = blocks.shape[:3]
    col_blocks = mesh.shape["tensor"] * width_dev // block_size
    my_seq = lax.axis_index("seq")
    seq_one = my_seq.reshape(1)
    q = queries[0]
    own = [a[0] for a in (cache_keys, stretch_keys, cache_values, stretch_values)]
    flat = blocks.reshape(row_blocks * kept, block_size, block_size)

    if mesh.shape["dp"] == 2 and mesh.shape["groups"] == 2 and row_blocks % 16 == 0 and width_dev >= 16 * HD and max(row_blocks, kept) <= block_size:
        unit = row_blocks // 16
        groups = lax.axis_index("groups")
        half = 8 * unit * my_seq
        relay = half + unit * (2 + 3 * groups)

        def piece(start, count, more=0):
            return lax.dynamic_slice_in_dim(flat, start * kept, count * kept + more, 0)

        heads = width_dev // (2 * HD)
        soon, last = heads // 4, heads // 8
        carried = jnp.pad(
            block_columns.astype(jnp.bfloat16), ((0, block_size - row_blocks), (0, block_size - kept))
        )
        near1 = swap(jnp.concatenate([piece(relay, unit), carried[None]], axis=0), "dp")
        near2 = swap(piece(relay + unit, 2 * unit), "dp")
        peer = peer_side(own)
        shared, peer[0] = lax.optimization_barrier((piece(half, 2 * unit, EXTRA), peer[0]))
        shared = swap(shared, "dp")
        attended = attention(seq_one, q, own, peer, 0, soon)
        near1, attended = lax.optimization_barrier((near1, attended))
        peer_columns = near1[unit * kept, :row_blocks, :kept].astype(jnp.int32)
        table = column_table(jnp.stack([block_columns, peer_columns]), col_blocks)
        far1 = swap(near1, "groups")
        near1_other = swap(near1, "seq")
        attended = attention(seq_one, q, own, peer, soon, heads - soon - last, attended)
        near2, far1, attended = lax.optimization_barrier((near2, far1, attended))
        far2 = swap(near2, "groups")
        near2_other = swap(near2, "seq")
        far1_other = swap(far1, "seq")
        attended = attention(seq_one, q, own, peer, heads - last, last, attended)
        other = 8 * unit * (1 - my_seq)

        def stage(plan, acc=None, columns=None):
            row_list, sources, pieces = [], [], [flat]
            for start, count, value in plan:
                for i in range(count):
                    row_list.append(start + i)
                    sources.append(((0, 0, True), (len(pieces), i * kept, False)))
                pieces.append(value)
            return projection(attended, table, jnp.stack(row_list), tuple(sources), pieces, kept, acc, columns)

        def relayed(base, group):
            return base + unit * (2 + 3 * group)

        (early,) = stage(
            (
                (relayed(half, groups), unit, near1),
                (relayed(half, groups) + unit, 2 * unit, near2),
                (relayed(half, 1 - groups), unit, far1),
                (relayed(other, groups), unit, near1_other),
                (relayed(other, groups) + unit, 2 * unit, near2_other),
                (relayed(other, 1 - groups), unit, far1_other),
            ),
        )
        shared, early = lax.optimization_barrier((shared, early))
        shared_other = swap(shared, "seq")
        far2, early = lax.optimization_barrier((far2, early))
        far2_other = swap(far2, "seq")
        plan = (
            (half, 2 * unit, shared),
            (relayed(half, 1 - groups) + unit, 2 * unit, far2),
            (other, 2 * unit, shared_other),
            (relayed(other, 1 - groups) + unit, 2 * unit, far2_other),
        )
        n = mesh.shape["tensor"]
        place = lax.axis_index("tensor")
        sums = {}
        for group in (sorted({n - 1, 1}), sorted(set(range(n)) - {n - 1, 1})):
            if group:
                columns = jnp.stack([(place + j) % n * row_blocks for j in group])
                found = stage(plan, early, columns)
                for i, j in enumerate(group):
                    sums[j] = found[2 * i : 2 * i + 2]
        return line_scatter(lambda j: sums[j], n)[None]
    else:
        dp = mesh.shape["dp"]
        gathered = lax.all_gather(flat, "dp", axis=0, tiled=True)
        table = column_table(lax.all_gather(block_columns, "dp", axis=0), col_blocks)
        peer = peer_side(own)
        attended = attention(seq_one, q, own, peer, 0, width_dev // (2 * HD))
        sources = tuple(tuple((0, d * row_blocks * kept, True) for d in range(dp)) for _ in range(row_blocks))
        (partial_value,) = projection(
            attended, table, jnp.arange(row_blocks, dtype=jnp.int32), sources, [gathered], kept
        )
    owned = lax.psum_scatter(partial_value, "tensor", scatter_dimension=1, tiled=True)
    return owned[None]


def solution(mesh):
    token = P(("groups", "dp"), "seq", "tensor")
    placed = (token, token, token, token, token, P("tensor", "dp", None, None), P("tensor", "dp"))
    return jax.shard_map(
        functools.partial(shards, mesh),
        mesh=mesh,
        in_specs=placed,
        out_specs=token,
        check_vma=False,
    )
```

```python
import functools
import math

import jax
import jax.numpy as jnp
from jax import lax
from jax.experimental import pallas as pl
from jax.experimental.pallas import tpu as pltpu
from jax.sharding import PartitionSpec as P

HD = 128
FLOOR = -1e30
TILE = 768
STEP_COLS = 16
EXTRA = 3


def in_hbm(value):
    return pltpu.with_memory_space_constraint(value, pltpu.HBM)


def attention_body(seq_ref, q_ref, cka, ska, ckb, skb, cva, sva, cvb, svb, out_ref):
    rows = q_ref.shape[0]
    cache_rows = cka.shape[0]
    scale = HD ** (-0.5) * math.log2(math.e)
    q = q_ref[...].astype(jnp.float32) * scale
    q_hi = q.astype(jnp.bfloat16)
    q_lo = (q - q_hi.astype(jnp.float32)).astype(jnp.bfloat16)
    q_two = jnp.concatenate(
        [jnp.concatenate([q_hi[:, h * HD : (h + 1) * HD], q_lo[:, h * HD : (h + 1) * HD]], axis=1) for h in range(2)],
        axis=0,
    )
    whole = (cache_rows - 1) // TILE
    tiles = []
    for side, (ck, sk, cv, sv) in enumerate(((cka, ska, cva, sva), (ckb, skb, cvb, svb))):
        for t in range(whole):
            tiles.append((ck, cv, None, None, t * TILE, (t + 1) * TILE, None))
        tiles.append((ck, cv, sk, sv, whole * TILE, cache_rows, side))

    def take(main, fresh, lo, hi):
        return main[lo:hi, :] if fresh is None else jnp.concatenate([main[lo:hi, :], fresh[...]], axis=0)

    def score(tile):
        ck, _, sk, _, lo, hi, side = tile
        keys = take(ck, sk, lo, hi)
        scores = lax.dot_general(
            q_two,
            jnp.concatenate([keys, keys], axis=1),
            (((1,), (1,)), ((), ())),
            preferred_element_type=jnp.float32,
        )
        if side is None:
            return scores
        tail = scores[:, hi - lo :]
        if side == 0:
            token = lax.broadcasted_iota(jnp.int32, (rows, rows), 0)
            position = lax.broadcasted_iota(jnp.int32, (rows, rows), 1)
            seen = position <= token
            tail = jnp.where(jnp.concatenate([seen, seen], axis=0), tail, FLOOR)
        else:
            tail = jnp.where(seq_ref[0] > 0, tail, FLOOR)
        return jnp.concatenate([scores[:, : hi - lo], tail], axis=1)

    peak = acc = None
    upcoming = score(tiles[0])
    for i, tile in enumerate(tiles):
        scores = upcoming
        if i + 1 < len(tiles):
            upcoming = score(tiles[i + 1])
        tile_peak = jnp.max(scores, axis=1, keepdims=True)
        new_peak = tile_peak if peak is None else jnp.maximum(peak, tile_peak)
        expo = jnp.exp2(scores - new_peak).astype(jnp.bfloat16)
        values = take(tile[1], tile[3], tile[4], tile[5])
        added = jnp.dot(
            expo,
            jnp.concatenate([values, jnp.ones_like(values)], axis=1),
            preferred_element_type=jnp.float32,
        )
        acc = added if acc is None else acc * jnp.exp2(peak - new_peak) + added
        peak = new_peak
    result = acc[:, :HD] / acc[:, HD:]
    out_ref[:, :HD] = result[:rows].astype(out_ref.dtype)
    out_ref[:, HD:] = result[rows:].astype(out_ref.dtype)


def attention(my_seq, q, own, peer, first, count, earlier=None):
    rows, width = q.shape
    ck, sk, cv, sv = own
    pck, psk, pcv, psv = peer
    cache_rows = ck.shape[0]
    qspec = pl.BlockSpec((rows, 2 * HD), lambda g, s: (0, g + first))
    cspec = pl.BlockSpec((cache_rows, HD), lambda g, s: (0, g + first))
    nspec = pl.BlockSpec((rows, HD), lambda g, s: (0, g + first))
    args = [q, ck, sk, pck, psk, cv, sv, pcv, psv]
    specs = [qspec, cspec, nspec, cspec, nspec, cspec, nspec, cspec, nspec]
    body = attention_body
    aliases = {}
    if earlier is not None:
        body = lambda *refs: attention_body(*refs[:10], *refs[11:])
        args.append(earlier)
        specs.append(pl.BlockSpec(memory_space=pltpu.HBM))
        aliases = {10: 0}
    return pl.pallas_call(
        body,
        out_shape=pltpu.HBM((rows, width), jnp.bfloat16),
        grid_spec=pltpu.PrefetchScalarGridSpec(
            num_scalar_prefetch=1,
            grid=(count,),
            in_specs=specs,
            out_specs=qspec,
        ),
        input_output_aliases=aliases,
        compiler_params=pltpu.CompilerParams(
            dimension_semantics=("arbitrary",), vmem_limit_bytes=20 << 20
        ),
        cost_estimate=pl.CostEstimate(flops=1, transcendentals=0, bytes_accessed=1),
        name="attention" if earlier is None else "late_attention",
    )(my_seq, *[in_hbm(a) for a in args])


def projection_body(sources, kept, has_acc, split, n_steps, table_ref, rows_ref, cols_ref, x_hbm, *refs):
    n_pieces = 1 + max(piece for row in sources for piece, _, _ in row)
    pieces, refs = refs[:n_pieces], refs[n_pieces:]
    if has_acc:
        acc_hbm, refs = refs[0], refs[1:]
    n_outs = 2 * n_steps if split else 1
    outs, refs = refs[:n_outs], refs[n_outs:]
    held, sems, stage, out_sems, x_ref, x_sem = refs[:6]
    slots = len(sources[0]) * kept
    empty = len(sources) * slots
    row_ids = [rows_ref[i] for i in range(len(sources))]
    step_cols = stage.shape[2] // HD
    span = step_cols * HD
    tokens = stage.shape[1]
    copies = [pltpu.make_async_copy(x_hbm, x_ref, x_sem)]
    for i, row in enumerate(sources):
        for j, (piece, offset, by_row) in enumerate(row):
            start = offset + row_ids[i] * kept if by_row else offset
            copies.append(
                pltpu.make_async_copy(
                    pieces[piece].at[pl.ds(start, kept)],
                    held.at[pl.ds(i * slots + j * kept, kept)],
                    sems.at[i, j],
                )
            )
    for copy in copies:
        copy.start()
    where = [pl.ds(pl.multiple_of(cols_ref[step] * HD, span), span) for step in range(n_steps)]
    fills = []
    if has_acc:
        acc_ref, acc_sems = refs[6:]
        for step in range(n_steps):
            fills.append(pltpu.make_async_copy(acc_hbm.at[:, where[step]], acc_ref.at[step], acc_sems.at[step]))
            fills[step].start()
    held[empty] = jnp.zeros(held.shape[1:], held.dtype)
    for copy in copies:
        copy.wait()
    x = jnp.concatenate([x_ref[:, pl.ds(pl.multiple_of(r * HD, HD), HD)] for r in row_ids], axis=1)
    drains = []
    for step in range(n_steps):
        slot = step % 2
        if split:
            half = tokens // 2
            drains.append(
                [
                    pltpu.make_async_copy(
                        stage.at[slot, pl.ds(side * half, half)], outs[2 * step + side], out_sems.at[slot, side]
                    )
                    for side in range(2)
                ]
            )
        else:
            drains.append([pltpu.make_async_copy(stage.at[slot], outs[0].at[:, where[step]], out_sems.at[slot, 0])])
        if step >= 2:
            for copy in drains[step - 2]:
                copy.wait()
        if has_acc:
            fills[step].wait()
        for pair in range(step_cols // 2):
            sides = []
            for side in range(2):
                col = cols_ref[step] + 2 * pair + side
                sides.append(
                    jnp.concatenate(
                        [held[jnp.minimum(table_ref[r, col] + i * slots, empty)] for i, r in enumerate(row_ids)],
                        axis=0,
                    )
                )
            value = jnp.dot(x, jnp.concatenate(sides, axis=1), preferred_element_type=jnp.float32)
            lanes = slice(2 * pair * HD, 2 * (pair + 1) * HD)
            if has_acc:
                value = value + acc_ref[step, :, lanes]
            stage[slot, :, lanes] = value.astype(stage.dtype)
        for copy in drains[step]:
            copy.start()
    for step in range(max(0, n_steps - 2), n_steps):
        for copy in drains[step]:
            copy.wait()


def projection(x, table, row_ids, sources, pieces, kept, acc=None, columns=None):
    tokens, width = x.shape
    col_blocks = table.shape[1]
    n_rows = len(sources)
    slots = len(sources[0]) * kept
    split = columns is not None
    if split:
        step_cols, n_steps = width // HD, columns.shape[0]
        out_shape = [pltpu.HBM((tokens // 2, width), x.dtype)] * (2 * n_steps)
    else:
        step_cols = min(STEP_COLS, col_blocks)
        n_steps = col_blocks // step_cols
        columns = jnp.arange(n_steps, dtype=jnp.int32) * step_cols
        out_shape = [pltpu.HBM((tokens, col_blocks * HD), x.dtype)]
    span = step_cols * HD
    smem = pl.BlockSpec(memory_space=pltpu.SMEM)
    hbm = pl.BlockSpec(memory_space=pl.ANY)
    scratch = [
        pltpu.VMEM((n_rows * slots + 1, HD, HD), x.dtype),
        pltpu.SemaphoreType.DMA((n_rows, len(sources[0]))),
        pltpu.VMEM((2, tokens, span), x.dtype),
        pltpu.SemaphoreType.DMA((2, 2)),
        pltpu.VMEM((tokens, width), x.dtype),
        pltpu.SemaphoreType.DMA(()),
    ]
    if acc is not None:
        scratch += [pltpu.VMEM((n_steps, tokens, span), x.dtype), pltpu.SemaphoreType.DMA((n_steps,))]
    return pl.pallas_call(
        functools.partial(projection_body, sources, kept, acc is not None, split, n_steps),
        out_shape=out_shape,
        in_specs=[smem, smem, smem, hbm] + [hbm] * len(pieces) + ([hbm] if acc is not None else []),
        out_specs=[hbm] * len(out_shape),
        scratch_shapes=scratch,
        compiler_params=pltpu.CompilerParams(vmem_limit_bytes=28 << 20),
        cost_estimate=pl.CostEstimate(flops=1, transcendentals=0, bytes_accessed=1),
        name="projection" if split else "early_projection",
    )(
        table,
        row_ids,
        columns,
        in_hbm(x),
        in_hbm(pieces[0]),
        *pieces[1:],
        *(() if acc is None else (in_hbm(acc),)),
    )


def add(*values):
    return sum(v.astype(jnp.float32) for v in values).astype(values[0].dtype)


def line_scatter(sent_first, parts, n):
    arrived = [None, None]
    for step in range(1, n):
        for half in range(2):
            up, down = parts[n - step][half], parts[step][half]
            if step == 1:
                up = down = sent_first[half]
            else:
                from_below, from_above = lax.optimization_barrier(arrived[half])
                up, down = add(up, from_below), add(down, from_above)
            arrived[half] = (
                lax.ppermute(up, "tensor", [(i, i + 1) for i in range(step)]),
                lax.ppermute(down, "tensor", [(i + 1, i) for i in range(n - 1 - step, n - 1)]),
            )
    return jnp.concatenate([add(parts[0][half], *arrived[half]) for half in range(2)], axis=0)


def swap(value, axis):
    return lax.ppermute(value, axis, [(0, 1), (1, 0)])


def after(value, *earlier):
    return lax.optimization_barrier((value,) + earlier)[0]


def peer_side(own):
    ck, sk, cv, sv = own
    return [swap(a, "seq") for a in (ck, sk, cv, sv)]


def column_table(all_columns, col_blocks):
    dp, _, kept = all_columns.shape
    slot = jnp.arange(dp, dtype=jnp.int32)[:, None] * kept + jnp.arange(kept, dtype=jnp.int32)[None, :]
    match = all_columns[..., None] == jnp.arange(col_blocks, dtype=jnp.int32)
    return jnp.min(jnp.where(match, slot[:, None, :, None], 1 << 20), axis=(0, 2))


def shards(mesh, queries, stretch_keys, stretch_values, cache_keys, cache_values, blocks, block_columns):
    width_dev = queries.shape[2]
    row_blocks, kept, block_size = blocks.shape[:3]
    col_blocks = mesh.shape["tensor"] * width_dev // block_size
    my_seq = lax.axis_index("seq")
    seq_one = my_seq.reshape(1)
    q = queries[0]
    own = [a[0] for a in (cache_keys, stretch_keys, cache_values, stretch_values)]
    flat = blocks.reshape(row_blocks * kept, block_size, block_size)

    if mesh.shape["dp"] == 2 and mesh.shape["groups"] == 2 and row_blocks % 16 == 0 and width_dev >= 16 * HD and max(row_blocks, kept) <= block_size:
        unit = row_blocks // 16
        groups = lax.axis_index("groups")
        half = 8 * unit * my_seq
        relay = half + unit * (2 + 3 * groups)

        def piece(start, count, more=0):
            return lax.dynamic_slice_in_dim(flat, start * kept, count * kept + more, 0)

        heads = width_dev // (2 * HD)
        soon, last = heads // 4, heads // 8
        carried = jnp.pad(
            block_columns.astype(jnp.bfloat16), ((0, block_size - row_blocks), (0, block_size - kept))
        )
        near1 = swap(jnp.concatenate([piece(relay, unit), carried[None]], axis=0), "dp")
        near2 = swap(piece(relay + unit, 2 * unit), "dp")
        peer = peer_side(own)
        shared, peer[0] = lax.optimization_barrier((piece(half, 2 * unit, EXTRA), peer[0]))
        shared = swap(shared, "dp")
        attended = attention(seq_one, q, own, peer, 0, soon)
        near1, attended = lax.optimization_barrier((near1, attended))
        peer_columns = near1[unit * kept, :row_blocks, :kept].astype(jnp.int32)
        table = column_table(jnp.stack([block_columns, peer_columns]), col_blocks)
        far1 = swap(near1, "groups")
        near1_other = swap(near1, "seq")
        attended = attention(seq_one, q, own, peer, soon, heads - soon - last, attended)
        near2, far1, attended = lax.optimization_barrier((near2, far1, attended))
        far2 = swap(near2, "groups")
        near2_other = swap(near2, "seq")
        far1_other = swap(far1, "seq")
        attended = attention(seq_one, q, own, peer, heads - last, last, attended)
        other = 8 * unit * (1 - my_seq)

        def stage(plan, acc=None, columns=None):
            row_list, sources, pieces = [], [], [flat]
            for start, count, value in plan:
                for i in range(count):
                    row_list.append(start + i)
                    sources.append(((0, 0, True), (len(pieces), i * kept, False)))
                pieces.append(value)
            return projection(attended, table, jnp.stack(row_list), tuple(sources), pieces, kept, acc, columns)

        def relayed(base, group):
            return base + unit * (2 + 3 * group)

        (early,) = stage(
            (
                (relayed(half, groups), unit, near1),
                (relayed(half, groups) + unit, 2 * unit, near2),
                (relayed(half, 1 - groups), unit, far1),
                (relayed(other, groups), unit, near1_other),
                (relayed(other, groups) + unit, 2 * unit, near2_other),
                (relayed(other, 1 - groups), unit, far1_other),
            ),
        )
        shared, early = lax.optimization_barrier((shared, early))
        shared_other = swap(shared, "seq")
        far2, early = lax.optimization_barrier((far2, early))
        far2_other = swap(far2, "seq")
        plan = (
            (half, 2 * unit, shared),
            (relayed(half, 1 - groups) + unit, 2 * unit, far2),
            (other, 2 * unit, shared_other),
            (relayed(other, 1 - groups) + unit, 2 * unit, far2_other),
        )
        n = mesh.shape["tensor"]
        place = lax.axis_index("tensor")
        ends = jnp.where(place == 0, (n - 1) * row_blocks, 0).astype(jnp.int32)
        sent_first = stage(plan, early, ends.reshape(1))
        found = stage(plan, early, jnp.stack([(place + j) % n * row_blocks for j in range(n)]))
        return line_scatter(sent_first, [found[2 * j : 2 * j + 2] for j in range(n)], n)[None]
    else:
        dp = mesh.shape["dp"]
        gathered = lax.all_gather(flat, "dp", axis=0, tiled=True)
        table = column_table(lax.all_gather(block_columns, "dp", axis=0), col_blocks)
        peer = peer_side(own)
        attended = attention(seq_one, q, own, peer, 0, width_dev // (2 * HD))
        sources = tuple(tuple((0, d * row_blocks * kept, True) for d in range(dp)) for _ in range(row_blocks))
        (partial_value,) = projection(
            attended, table, jnp.arange(row_blocks, dtype=jnp.int32), sources, [gathered], kept
        )
    owned = lax.psum_scatter(partial_value, "tensor", scatter_dimension=1, tiled=True)
    return owned[None]


def solution(mesh):
    token = P(("groups", "dp"), "seq", "tensor")
    placed = (token, token, token, token, token, P("tensor", "dp", None, None), P("tensor", "dp"))
    return jax.shard_map(
        functools.partial(shards, mesh),
        mesh=mesh,
        in_specs=placed,
        out_specs=token,
        check_vma=False,
    )
```
